512 devices in a mesh: row: 16 (over y, core), col: 32 (over x, z).
Axes of the slice: x: 4, y: 8, z: 8, core: 2. Of those that a mesh axis runs over, the one named last changes fastest.
Arguments:
- inverse_block: bfloat16 [16384, 16384], P('row', 'col'), may hold values from -0.375 to 0.375
- tile_mask: int32 [128, 128], P('row', 'col'), may hold values 0 or 1
- factor: bfloat16 [2, 16384, 256], P(None, 'row'), may hold values from -0.29882812 to 0.29882812
- panel_mask: int32 [2, 128], P(None, 'row'), may hold values 0 or 1
- child_top: bfloat16 [256, 256], replicated, may hold values from -0.375 to 0.375
- pivots: float32 [2, 256, 256], replicated, may hold values from -6 to 6
Outputs:
- parent_column: float32 [16384, 256], P(('row', 'col'))
- parent_diag: float32 [256, 256], replicated
- child_upper: float32 [256, 256], replicated
- child_column: float32 [16384, 256], P(('row', 'col'))
- child_diag: float32 [256, 256], replicated
The draws below stay inside these ranges and needn't reach their ends.
All inputs are finite; a program needn't handle non-finite values. No bound on the sum of `tile_mask` or of `panel_mask` on one device may be relied on, other than what follows from the above.
Results may differ from the reference program's by a relative error of at most 0.0003.
Values may be sent and summed in bfloat16 or wider, within the bound.
No kernel may reach another device: no remote copies, remote signals or barrier semaphores. Data moves between devices by JAX's collectives and lax.ppermute only.
A program may use at most 64 MiB of HBM per device.

```python
import jax
import jax.numpy as jnp
from jax import lax

W = 256
BLOCK = 128
R = 16384


def set_ends(array, stream_key, smallest, largest):
    extent = array.shape
    place = [jax.random.randint(jax.random.fold_in(stream_key, axis), (), 0, extent[axis]) for axis in range(len(extent))]
    array = array.at[tuple(place)].set(smallest)
    longest = extent.index(max(extent))
    place[longest] = (place[longest] + 1) % extent[longest]
    return array.at[tuple(place)].set(largest)


def block_scale(stream_key, shape, split, smallest, largest):
    def one(position, parts):
        draws = jax.random.uniform(jax.random.fold_in(jax.random.fold_in(stream_key, 6), position), (parts,), jnp.float32, smallest / len(split), largest / len(split))
        return jnp.repeat(jnp.exp(draws), shape[position] // parts).reshape((-1,) + (1,) * (len(shape) - position - 1))

    factor_of = one(*split[0])
    for cut in split[1:]:
        factor_of = factor_of * one(*cut)
    return factor_of


def centred(own_key, extent, scale, reach, shards=(), held_as=jnp.bfloat16):
    loudness = block_scale(own_key, extent, shards, -0.22, 0.18) if shards else 1.0
    result = jax.random.normal(own_key, extent, jnp.float32) * scale * loudness
    return jnp.minimum(jnp.maximum(result, -reach), reach).astype(held_as)


def setup_inputs(seed: int = 0) -> dict:
    key_list = jax.random.split(jax.random.key(seed), 7)
    return {
        "inverse_block": centred(key_list[0], (R, R), (R // 64) ** -0.5, 0.375, ((0, 16), (1, 32))),
        "tile_mask": set_ends((jax.random.randint(key_list[1], (R // BLOCK, R // BLOCK), 0, 5) < 3).astype(jnp.int32), jax.random.fold_in(key_list[1], 1), 0, 1),
        "factor": centred(key_list[2], (2, R, W), 0.05, 0.29882812, ((1, 16),)),
        "panel_mask": set_ends((jax.random.randint(key_list[3], (2, R // BLOCK), 0, 5) < 3).astype(jnp.int32), jax.random.fold_in(key_list[3], 1), 0, 1),
        "child_top": centred(key_list[4], (W, W), W ** -0.5, 0.375),
        "pivots": centred(key_list[5], (2, W, W), 1.0, 6.0, (), jnp.float32),
    }


def reference(inverse_block, tile_mask, factor, panel_mask, child_top, pivots):
    total_rows = inverse_block.shape[0]
    panel_width = factor.shape[2]
    nblocks = total_rows // 128
    keep_panel = panel_mask.astype(jnp.bfloat16)
    panels = (factor.reshape(2, nblocks, 128, panel_width) * keep_panel[:, :, None, None]).reshape(2, total_rows, panel_width)
    joined_panels = jnp.concatenate([panels[0], panels[1]], axis=1)
    slab_rows = 1024
    slab_count = total_rows // slab_rows

    def one_slab(slab_index):
        slab = lax.dynamic_slice_in_dim(inverse_block, slab_index * slab_rows, slab_rows, 0)
        slab_mask = lax.dynamic_slice_in_dim(tile_mask, slab_index * (slab_rows // 128), slab_rows // 128, 0)
        masked = (slab.reshape(slab_rows // 128, 128, nblocks, 128) * slab_mask.astype(jnp.bfloat16)[:, None, :, None]).reshape(slab_rows, total_rows)
        return jnp.dot(masked, joined_panels, preferred_element_type=jnp.float32)

    products = lax.map(one_slab, jnp.arange(slab_count, dtype=jnp.int32)).reshape(total_rows, 2 * panel_width)
    highest = lax.Precision.HIGHEST
    panel_zero = panels[0].astype(jnp.float32)
    panel_one = panels[1].astype(jnp.float32)
    top_float = child_top.astype(jnp.float32)
    parent_column = -products[:, :panel_width]
    parent_diag = pivots[0] - jnp.dot(panel_zero.T, parent_column, precision=highest)
    child_upper = -(jnp.dot(parent_diag, top_float, precision=highest) + jnp.dot(parent_column.T, panel_one, precision=highest))
    child_column = -(jnp.dot(parent_column, top_float, precision=highest) + products[:, panel_width:])
    child_diag = pivots[1] - jnp.dot(top_float.T, child_upper, precision=highest) - jnp.dot(panel_one.T, child_column, precision=highest)
    return parent_column, parent_diag, child_upper, child_column, child_diag
```

```python
import jax
import jax.numpy as jnp
from jax import lax
from jax.sharding import Mesh, PartitionSpec as P

ROW = ("y", "core")
COL = ("x", "z")
HIGHEST = lax.Precision.HIGHEST
LIMIT = 32766.0


def mm(a, b, ca, cb):
    return lax.dot_general(
        a, b, (((ca,), (cb,)), ((), ())), precision=HIGHEST, preferred_element_type=jnp.float32
    )


def scale_of(value, axes):
    top = jnp.maximum(jnp.max(jnp.abs(value), axis=axes, keepdims=True), 1e-30)
    power = jnp.ceil(jnp.log2(top))
    mantissa = jnp.ceil(top * jnp.exp2(14.0 - power) + 2.0)
    code = (power.astype(jnp.int32) << 16) | mantissa.astype(jnp.int32)
    return mantissa * jnp.exp2(power - 14.0), code


def scale_from(code):
    return (code & 0xFFFF).astype(jnp.float32) * jnp.exp2((code >> 16).astype(jnp.float32) - 14.0)


def join(high, low):
    return (high << 16) | (low & 0xFFFF)


def part(joined):
    return joined >> 16, (joined << 16) >> 16


def exchange(partial, axis):
    rows = partial.shape[3]
    step, code = scale_of(partial, (3,))
    whole = jnp.round(partial * (LIMIT / step)).astype(jnp.int32)
    body = join(whole[0], whole[1])
    lane = lax.broadcasted_iota(jnp.int32, body.shape[:2] + (128,), 2)
    code = jnp.where(lane < 64, code[0], code[1])
    got = lax.all_to_all(jnp.concatenate([body, code], axis=2), axis, 0, 0, tiled=True)
    step = scale_from(jnp.stack([got[:, :, rows], got[:, :, rows + 64]])) * (1.0 / LIMIT)
    whole = jnp.stack(part(got[:, :, :rows])).astype(jnp.float32)
    return jnp.sum(whole * step[..., None], axis=1)


def shards(inverse_block, tile_mask, factor, panel_mask, child_top, pivots):
    rows, cols = inverse_block.shape
    width = factor.shape[2]
    ny, ncore = lax.axis_size("y"), lax.axis_size("core")
    nrow = ny * ncore
    nx, nz = lax.axis_size("x"), lax.axis_size("z")
    ncol = nx * nz
    core = lax.axis_index("core")
    col = lax.axis_index(COL)
    halves = rows // cols
    piece = cols // nrow
    own_rows = rows // ncol
    slot = width // ncol

    pairs = []
    for s in range(nrow):
        for q in range(ncol):
            r, h = q // halves, q % halves
            pairs.append((s * ncol + q, r * ncol + halves * s + h))
    to_row, half = col // halves, col % halves
    start = half * cols + (to_row % ncore) * (cols // ncore) + (to_row // ncore) * piece
    sent = lax.dynamic_slice_in_dim(factor, start, piece, 1)
    kept = lax.dynamic_slice_in_dim(panel_mask, start // 128, 1, 1)[:, :, None]
    sent = jnp.where(kept == 1, sent, 0).astype(jnp.bfloat16)
    sent = jnp.concatenate([sent[0], sent[1]], axis=1)
    mine = lax.ppermute(sent, ROW + COL, pairs)
    same = lax.all_to_all(
        jnp.broadcast_to(mine[None], (ny,) + mine.shape), "y", 0, 0, tiled=True
    ).reshape(cols // ncore, 2 * width)
    other = lax.ppermute(same, "core", [(0, 1), (1, 0)])
    first = jnp.where(core == 0, same, other)
    second = jnp.where(core == 0, other, same)
    panel = jnp.concatenate([first, second], axis=0)

    keep = panel_mask.astype(jnp.bfloat16)
    panels = (
        factor.reshape(2, rows // 128, 128, width) * keep[:, :, None, None]
    ).reshape(2, rows, width)
    joined = jnp.concatenate([panels[0], panels[1]], axis=1).astype(jnp.float32)

    mask = tile_mask.astype(jnp.bfloat16)[:, None, :, None]
    masked = (inverse_block.reshape(rows // 128, 128, cols // 128, 128) * mask).reshape(rows, cols)
    partial = lax.dot_general(
        panel, masked, (((0,), (1,)), ((), ())), preferred_element_type=jnp.float32
    )
    total = exchange(partial.reshape(2, nx, nz * slot, rows), "x")
    total = exchange(total.reshape(2, nz, slot, rows), "z")

    gram_parent = mm(total[0], joined, 1, 0)
    gram_child = mm(total[1], joined[:, width:], 1, 0)
    gram = jnp.concatenate([gram_parent[:, :width], gram_parent[:, width:], gram_child], axis=0)
    gram = gram + lax.ppermute(gram, "core", [(0, 1), (1, 0)])
    spread = lax.all_to_all(jnp.broadcast_to(gram[None], (ny,) + gram.shape), "y", 0, 0, tiled=True)
    gram = jnp.sum(spread.reshape((ny, 3, slot, width)), axis=0)

    step, code = scale_of(gram, (1, 2))
    whole = jnp.round(gram * (LIMIT / step)).astype(jnp.int32)
    packed = join(whole[:, :, : width // 2], whole[:, :, width // 2 :]).reshape(3 * slot, width // 2)
    row_step, row_code = scale_of(total, (0, 1, 2))
    fixed = jnp.round(total * (float(1 << 30) / row_step)).astype(jnp.int32)
    fixed = fixed.reshape(2, slot // 2, 2, nx, nz, own_rows).transpose(3, 4, 1, 2, 0, 5)
    fixed = fixed.reshape(ncol, slot // 2, 128)
    codes = jnp.broadcast_to(
        jnp.concatenate([code.reshape(3, 1), row_code.reshape(1, 1)]), (4, 128)
    )
    same_for_all = jnp.concatenate([packed, codes], axis=0)
    same_for_all = jnp.broadcast_to(same_for_all[None], (ncol,) + same_for_all.shape)
    last = lax.all_to_all(jnp.concatenate([same_for_all, fixed], axis=1), COL, 0, 0, tiled=True)
    scales = scale_from(last[:, 3 * slot : 3 * slot + 4, :])
    high, low = part(last[:, : 3 * slot].reshape(ncol, 3, slot, width // 2))
    unit = scales[:, :3, :1, None] * (1.0 / LIMIT)
    grams = jnp.concatenate([high.astype(jnp.float32) * unit, low.astype(jnp.float32) * unit], axis=3)
    grams = grams.transpose(1, 0, 2, 3).reshape(3, width, width)
    sums = last[:, 3 * slot + 4 :].astype(jnp.float32) * (scales[:, 3:4, :1] * (1.0 / (1 << 30)))
    sums = sums.reshape(ncol, slot // 2, 2, 2, own_rows).transpose(3, 4, 0, 1, 2).reshape(2, own_rows, width)

    top = child_top.astype(jnp.float32)
    parent_column = -sums[0]
    child_column = -(mm(parent_column, top, 1, 0) + sums[1])
    parent_diag = pivots[0] + grams[0].T
    child_upper = mm(-parent_diag, top, 1, 0) + grams[1]
    child_diag = pivots[1] - mm(top, child_upper, 0, 0) - mm(grams[1], top, 0, 0) + grams[2].T
    return (parent_column, parent_diag, child_upper, child_column, child_diag)


def solution(mesh):
    grid = Mesh(mesh.devices.reshape(8, 2, 4, 8), ROW + COL)
    in_specs = (P(ROW, COL), P(ROW, COL), P(None, ROW, None), P(None, ROW), P(), P())
    out_specs = (P(ROW + COL, None), P(), P(), P(ROW + COL, None), P())
    return jax.shard_map(shards, mesh=grid, in_specs=in_specs, out_specs=out_specs, check_vma=False)
```

```python
import jax
import jax.numpy as jnp
from jax import lax
from jax.experimental import pallas as pl
from jax.experimental.pallas import tpu as pltpu
from jax.sharding import Mesh, PartitionSpec as P

ROW = ("y", "core")
COL = ("x", "z")
LIMIT = 32766.0
FIXED = float(1 << 30)
VMEM = pl.BlockSpec(memory_space=pltpu.VMEM)
SMEM = pl.BlockSpec(memory_space=pltpu.SMEM)


def scale_of(top):
    top = jnp.maximum(top, 1e-30)
    power = jnp.ceil(jnp.log2(top))
    mantissa = jnp.ceil(top * jnp.exp2(14.0 - power) + 2.0)
    code = (power.astype(jnp.int32) << 16) | mantissa.astype(jnp.int32)
    return mantissa * jnp.exp2(power - 14.0), code


def scale_from(code):
    return (code & 0xFFFF).astype(jnp.float32) * jnp.exp2((code >> 16).astype(jnp.float32) - 14.0)


def whole(value, factor):
    return jnp.round(value * factor).astype(jnp.int32)


def join(high, low):
    return (high << 16) | (low & 0xFFFF)


def part(joined):
    return (joined >> 16).astype(jnp.float32), ((joined << 16) >> 16).astype(jnp.float32)


def split(value):
    high = value.astype(jnp.bfloat16)
    rest = value - high.astype(jnp.float32)
    middle = rest.astype(jnp.bfloat16)
    return high, middle, (rest - middle.astype(jnp.float32)).astype(jnp.bfloat16)


def dot(a, b, ca, cb):
    return lax.dot_general(a, b, (((ca,), (cb,)), ((), ())), preferred_element_type=jnp.float32)


def encode_rows(high, low):
    high_step, high_code = scale_of(jnp.max(jnp.abs(high), axis=1, keepdims=True))
    low_step, low_code = scale_of(jnp.max(jnp.abs(low), axis=1, keepdims=True))
    body = join(whole(high, LIMIT / high_step), whole(low, LIMIT / low_step))
    lane = lax.broadcasted_iota(jnp.int32, (high.shape[0], 128), 1)
    return body, jnp.where(lane < 64, high_code, low_code)


def decode_rows(ref, index, rows):
    high, low = part(ref[index, :, :rows])
    code = ref[index, :, rows:]
    return high * (scale_from(code[:, :1]) * (1.0 / LIMIT)), low * (scale_from(code[:, 64:65]) * (1.0 / LIMIT))


def piece_kernel(at_ref, mask_ref, factor_ref, out_ref):
    width = factor_ref.shape[2]
    block = at_ref[0] * factor_ref.shape[1] // 128
    for k in range(2):
        kept = jnp.where(mask_ref[k, block] == 1, factor_ref[k], 0.0)
        out_ref[:, k * width : k * width + width] = kept.astype(jnp.bfloat16)


def product_kernel(mask_ref, core_ref, same_ref, other_ref, inverse_ref, out_ref, turned, product):
    width = same_ref.shape[1] // 2
    rows, cols = inverse_ref.shape
    first = core_ref[0] == 0
    turned[:, : cols // 2] = jnp.where(first, same_ref[...], other_ref[...]).T
    turned[:, cols // 2 :] = jnp.where(first, other_ref[...], same_ref[...]).T
    step = 256
    for i in range(rows // step):
        blocks = []
        for j in range(cols // 128):
            column = [
                jnp.where(
                    mask_ref[i * step // 128 + h, j] == 1,
                    inverse_ref[i * step + h * 128 : i * step + h * 128 + 128, j * 128 : j * 128 + 128],
                    0.0,
                ).astype(jnp.bfloat16)
                for h in range(step // 128)
            ]
            blocks.append(jnp.concatenate(column, axis=0))
        masked = jnp.concatenate(blocks, axis=1)
        product[:, i * step : i * step + step] = dot(turned[...], masked, 1, 1)
    count = out_ref.shape[1]
    for x in range(out_ref.shape[0]):
        body, code = encode_rows(
            product[x * count : x * count + count, :],
            product[width + x * count : width + x * count + count, :],
        )
        out_ref[x, :, :rows] = body
        out_ref[x, :, rows:] = code


def middle_kernel(in_ref, out_ref):
    rows = in_ref.shape[2] - 128
    high, low = decode_rows(in_ref, 0, rows)
    for i in range(1, in_ref.shape[0]):
        more_high, more_low = decode_rows(in_ref, i, rows)
        high, low = high + more_high, low + more_low
    body, code = encode_rows(high, low)
    out_ref[:, :rows] = body
    out_ref[:, rows:] = code


def encode_grams(grams, store):
    for k, gram in enumerate(grams):
        half = gram.shape[1] // 2
        top = jnp.max(jnp.max(jnp.abs(gram), axis=1, keepdims=True), axis=0, keepdims=True)
        step, code = scale_of(jnp.broadcast_to(top, (1, half)))
        inverse = LIMIT / step
        store(k, join(whole(gram[:, :half], inverse), whole(gram[:, half:], inverse)), code)


def gram_kernel(mask_ref, in_ref, factor_ref, out_ref, total_ref):
    rows = in_ref.shape[2] - 128
    slot = in_ref.shape[1]
    high, low = decode_rows(in_ref, 0, rows)
    for i in range(1, in_ref.shape[0]):
        more_high, more_low = decode_rows(in_ref, i, rows)
        high, low = high + more_high, low + more_low
    total_ref[0], total_ref[1] = high, low
    pieces = jnp.concatenate([p.astype(jnp.float32) for p in split(high) + split(low)], axis=0)
    pieces = pieces.astype(jnp.bfloat16)
    sums = []
    for k in range(2):
        panel = jnp.concatenate(
            [
                jnp.where(mask_ref[k, i] == 1, factor_ref[k, i * 128 : i * 128 + 128, :], 0.0).astype(jnp.bfloat16)
                for i in range(rows // 128)
            ],
            axis=0,
        )
        found = dot(pieces, panel, 1, 0)
        for s in range(2):
            b = 3 * slot * s
            sums.append(
                found[b : b + slot] + found[b + slot : b + 2 * slot] + found[b + 2 * slot : b + 3 * slot]
            )
    half = sums[0].shape[1] // 2

    def store(k, body, code):
        for r in range(out_ref.shape[0]):
            out_ref[r, k * slot : k * slot + slot, :] = body
            out_ref[r, 3 * slot + k : 3 * slot + k + 1, :] = code

    filler = jnp.zeros((out_ref.shape[1] - 3 * slot - 3, half), jnp.int32)
    for r in range(out_ref.shape[0]):
        out_ref[r, 3 * slot + 3 :, :] = filler
    encode_grams((sums[0], sums[2], sums[3]), store)


def decode_gram(ref, index, k, slot):
    high, low = part(ref[index, k * slot : k * slot + slot, :])
    unit = scale_from(ref[index, 3 * slot + k : 3 * slot + k + 1, :]) * (1.0 / LIMIT)
    return jnp.concatenate([high * unit, low * unit], axis=1)


def spread_kernel(in_ref, fixed_ref, code_ref, out_ref):
    slot = (in_ref.shape[1] - 8) // 3
    grams = []
    for k in range(3):
        gram = decode_gram(in_ref, 0, k, slot)
        for i in range(1, in_ref.shape[0]):
            gram = gram + decode_gram(in_ref, i, k, slot)
        grams.append(gram)

    def store(k, body, code):
        for c in range(out_ref.shape[0]):
            out_ref[c, k * slot : k * slot + slot, :] = body
            out_ref[c, 3 * slot + k : 3 * slot + k + 1, :] = code

    encode_grams(grams, store)
    for c in range(out_ref.shape[0]):
        out_ref[c, 3 * slot + 3 : 3 * slot + 4, :] = code_ref[...]
        out_ref[c, 3 * slot + 4 :, :] = fixed_ref[c]


def exact(a, b, ca, cb):
    parts = split(a)
    return dot(parts[0], b, ca, cb) + (dot(parts[1], b, ca, cb) + dot(parts[2], b, ca, cb))


def final_kernel(in_ref, top_ref, pivots_ref, parent_column, parent_diag, child_upper, child_column, child_diag):
    ncol = in_ref.shape[0]
    width = top_ref.shape[0]
    slot = width // ncol
    top = top_ref[...]
    grams = []
    for k in range(3):
        high, low = part(in_ref[:, k * slot : k * slot + slot, :])
        unit = scale_from(in_ref[:, 3 * slot + k : 3 * slot + k + 1, :]) * (1.0 / LIMIT)
        high = (high * unit).reshape(width, width // 2)
        grams.append(jnp.concatenate([high, (low * unit).reshape(width, width // 2)], axis=1))
    diag = pivots_ref[0] + grams[0].T
    parent_diag[...] = diag
    upper = grams[1] - exact(diag, top, 1, 0)
    child_upper[...] = upper
    parts = split(upper)
    turned = dot(top, parts[0], 0, 0) + (dot(top, parts[1], 0, 0) + dot(top, parts[2], 0, 0))
    child_diag[...] = pivots_ref[1] - turned - exact(grams[1], top, 0, 0) + grams[2].T

    unit = scale_from(in_ref[:, 3 * slot + 3 : 3 * slot + 4, :]) * (1.0 / FIXED)
    count = ncol * slot // 2
    sums = (in_ref[:, 3 * slot + 4 :, :].astype(jnp.float32) * unit).reshape(count, 128)
    row = lax.broadcasted_iota(jnp.int32, (count, width), 0)
    column = lax.broadcasted_iota(jnp.int32, (count, width), 1)
    placed = None
    for h in range(2):
        choice = jnp.where(column == 2 * row + h, 1.0, 0.0).astype(jnp.bfloat16)
        for piece in split(sums):
            term = dot(piece, choice, 0, 0)[64 * h : 64 * h + 64]
            placed = term if placed is None else placed + term
    own = placed.shape[0] // 2
    parent_column[...] = -placed[:own]
    child_column[...] = exact(placed[:own], top, 1, 0) - placed[own:]


def call(kernel, out_shape, smem=0, scratch=(), results=pltpu.VMEM, name=None):
    single = isinstance(out_shape, jax.ShapeDtypeStruct)
    shapes = [out_shape] if single else list(out_shape)
    if results is not None:
        shapes = [results(s.shape, s.dtype) for s in shapes]

    def run(*args):
        found = pl.pallas_call(
            kernel,
            out_shape=shapes,
            in_specs=[SMEM] * smem + [VMEM] * (len(args) - smem),
            out_specs=[VMEM] * len(shapes),
            scratch_shapes=list(scratch),
            name=name,
        )(*args[:smem], *(pltpu.with_memory_space_constraint(a, pltpu.VMEM) for a in args[smem:]))
        return found[0] if single else found

    return run


def shards(inverse_block, tile_mask, factor, panel_mask, child_top, pivots):
    rows, cols = inverse_block.shape
    width = factor.shape[2]
    ncore = lax.axis_size("core")
    nrow = lax.axis_size("y") * ncore
    nx, nz = lax.axis_size("x"), lax.axis_size("z")
    ncol = nx * nz
    col = lax.axis_index(COL)
    halves = rows // cols
    piece = cols // nrow
    own_rows = rows // ncol
    slot = width // ncol
    i32 = lambda *shape: jax.ShapeDtypeStruct(shape, jnp.int32)
    f32 = lambda *shape: jax.ShapeDtypeStruct(shape, jnp.float32)

    pairs = []
    for s in range(nrow):
        for q in range(ncol):
            r, h = q // halves, q % halves
            pairs.append((s * ncol + q, r * ncol + halves * s + h))
    to_row = col // halves
    at = (col % halves) * nrow + (to_row % ncore) * (nrow // ncore) + to_row // ncore
    sent = pl.pallas_call(
        piece_kernel,
        out_shape=pltpu.VMEM((piece, 2 * width), jnp.bfloat16),
        grid_spec=pltpu.PrefetchScalarGridSpec(
            num_scalar_prefetch=2,
            grid=(1,),
            in_specs=[pl.BlockSpec((2, piece, width), lambda i, at, mask: (0, at[0], 0))],
            out_specs=VMEM,
        ),
        name="piece",
    )(at.reshape(1), panel_mask, factor)
    mine = lax.ppermute(sent, ROW + COL, pairs)
    same = lax.all_to_all(
        jnp.broadcast_to(mine[None], (nrow // ncore,) + mine.shape), "y", 0, 0, tiled=True
    ).reshape(cols // ncore, 2 * width)
    other = lax.ppermute(same, "core", [(0, 1), (1, 0)])

    coded = call(
        product_kernel,
        i32(nx, nz * slot, rows + 128),
        smem=2,
        scratch=[pltpu.VMEM((2 * width, cols), jnp.bfloat16), pltpu.VMEM((2 * width, rows), jnp.float32)],
        name="product",
    )(tile_mask, lax.axis_index("core").reshape(1), same, other, inverse_block)
    coded = lax.all_to_all(coded, "x", 0, 0, tiled=True)
    coded = call(middle_kernel, i32(nz * slot, rows + 128), name="middle")(coded)
    coded = lax.all_to_all(coded.reshape(nz, slot, rows + 128), "z", 0, 0, tiled=True)
    gram, total = call(
        gram_kernel, (i32(nrow, 3 * slot + 8, width // 2), f32(2, slot, rows)), smem=1, name="gram"
    )(panel_mask, coded, factor)
    gram = lax.all_to_all(gram, ROW, 0, 0, tiled=True)

    row_step, row_code = scale_of(jnp.max(jnp.abs(total)))
    fixed = whole(total, FIXED / row_step)
    fixed = fixed.reshape(2, slot // 2, 2, nx, nz, own_rows).transpose(3, 4, 1, 2, 0, 5)
    fixed = fixed.reshape(ncol, slot // 2, 128)
    last = call(spread_kernel, i32(ncol, 3 * slot + 8, width // 2), name="spread")(
        gram, fixed, jnp.broadcast_to(row_code, (1, 128))
    )
    last = lax.all_to_all(last, COL, 0, 0, tiled=True)
    return tuple(
        call(
            final_kernel,
            (f32(own_rows, width), f32(width, width), f32(width, width), f32(own_rows, width), f32(width, width)),
            results=None,
            name="final",
        )(last, child_top, pivots)
    )


def solution(mesh):
    grid = Mesh(mesh.devices.reshape(8, 2, 4, 8), ROW + COL)
    in_specs = (P(ROW, COL), P(ROW, COL), P(None, ROW, None), P(None, ROW), P(), P())
    out_specs = (P(ROW + COL, None), P(), P(), P(ROW + COL, None), P())
    return jax.shard_map(shards, mesh=grid, in_specs=in_specs, out_specs=out_specs, check_vma=False)
```

```python
import jax
import jax.numpy as jnp
from jax import lax
from jax.experimental import pallas as pl
from jax.experimental.pallas import tpu as pltpu
from jax.sharding import Mesh, PartitionSpec as P

ROW = ("y", "core")
COL = ("x", "z")
LIMIT = 32766.0
FIXED = float(1 << 30)
VMEM = pl.BlockSpec(memory_space=pltpu.VMEM)
SMEM = pl.BlockSpec(memory_space=pltpu.SMEM)


def scale_of(top):
    top = jnp.maximum(top, 1e-30)
    power = jnp.ceil(jnp.log2(top))
    mantissa = jnp.ceil(top * jnp.exp2(14.0 - power) + 2.0)
    code = (power.astype(jnp.int32) << 16) | mantissa.astype(jnp.int32)
    return mantissa * jnp.exp2(power - 14.0), code


def scale_from(code):
    return (code & 0xFFFF).astype(jnp.float32) * jnp.exp2((code >> 16).astype(jnp.float32) - 14.0)


def whole(value, factor):
    return jnp.round(value * factor).astype(jnp.int32)


def join(high, low):
    return (high << 16) | (low & 0xFFFF)


def part(joined):
    return (joined >> 16).astype(jnp.float32), ((joined << 16) >> 16).astype(jnp.float32)


def split(value):
    high = value.astype(jnp.bfloat16)
    rest = value - high.astype(jnp.float32)
    middle = rest.astype(jnp.bfloat16)
    return high, middle, (rest - middle.astype(jnp.float32)).astype(jnp.bfloat16)


def dot(a, b, ca, cb):
    return lax.dot_general(a, b, (((ca,), (cb,)), ((), ())), preferred_element_type=jnp.float32)


def encode_rows(high, low):
    high_step, high_code = scale_of(jnp.max(jnp.abs(high), axis=1, keepdims=True))
    low_step, low_code = scale_of(jnp.max(jnp.abs(low), axis=1, keepdims=True))
    body = join(whole(high, LIMIT / high_step), whole(low, LIMIT / low_step))
    lane = lax.broadcasted_iota(jnp.int32, (high.shape[0], 128), 1)
    return body, jnp.where(lane < 64, high_code, low_code)


def decode_rows(ref, index, rows):
    high, low = part(ref[index, :, :rows])
    code = ref[index, :, rows:]
    return high * (scale_from(code[:, :1]) * (1.0 / LIMIT)), low * (scale_from(code[:, 64:65]) * (1.0 / LIMIT))


SERVES = [
    [18, 23, 17, 15, 5, 0, 24, 22, 20, 21, 8, 11, 7, 4, 31, 12, 14, 13, 9, 29, 3, 2, 28, 10, 16, 19, 27, 25, 1, 6, 30, 26],
    [22, 16, 8, 21, 25, 13, 11, 4, 6, 14, 20, 19, 29, 5, 3, 30, 28, 26, 12, 15, 9, 31, 1, 0, 10, 24, 18, 17, 23, 27, 7, 2],
    [29, 12, 18, 26, 22, 19, 21, 13, 11, 8, 14, 24, 28, 25, 17, 1, 7, 6, 2, 10, 9, 27, 31, 4, 5, 0, 30, 16, 20, 23, 15, 3],
    [13, 3, 29, 10, 16, 26, 19, 21, 17, 1, 5, 4, 18, 14, 22, 27, 15, 11, 7, 6, 2, 12, 20, 25, 31, 8, 9, 0, 28, 30, 24, 23],
    [24, 27, 3, 13, 9, 12, 2, 30, 26, 25, 23, 17, 1, 18, 0, 8, 20, 29, 21, 19, 15, 6, 14, 28, 22, 31, 5, 11, 7, 10, 4, 16],
    [2, 6, 24, 27, 1, 5, 13, 10, 0, 26, 25, 28, 23, 29, 14, 16, 7, 22, 30, 3, 21, 19, 9, 12, 4, 18, 20, 31, 17, 15, 11, 8],
    [11, 8, 4, 2, 28, 29, 1, 5, 9, 16, 6, 26, 30, 25, 31, 7, 13, 10, 22, 0, 14, 27, 21, 17, 15, 12, 18, 20, 24, 3, 23, 19],
    [25, 5, 9, 14, 4, 6, 30, 29, 23, 3, 13, 10, 11, 28, 2, 31, 27, 21, 17, 18, 20, 22, 0, 26, 7, 19, 15, 12, 8, 24, 16, 1],
    [30, 3, 23, 25, 19, 18, 14, 8, 2, 7, 29, 13, 17, 20, 10, 6, 4, 5, 31, 27, 11, 16, 22, 26, 0, 9, 1, 21, 15, 12, 24, 28],
    [14, 24, 30, 7, 25, 23, 17, 16, 10, 2, 12, 31, 11, 9, 15, 22, 26, 0, 4, 1, 5, 29, 13, 8, 18, 28, 6, 3, 27, 21, 19, 20],
    [23, 22, 26, 18, 10, 11, 25, 19, 21, 20, 14, 2, 4, 13, 17, 15, 31, 12, 16, 30, 6, 5, 7, 9, 27, 24, 28, 8, 0, 3, 1, 29],
    [13, 19, 21, 20, 24, 28, 10, 3, 15, 16, 25, 22, 14, 0, 4, 5, 11, 29, 27, 12, 30, 9, 6, 2, 1, 31, 17, 26, 18, 23, 8, 7],
    [8, 15, 7, 1, 31, 22, 28, 16, 4, 20, 3, 21, 25, 26, 24, 0, 10, 9, 13, 5, 23, 27, 18, 6, 14, 11, 30, 19, 29, 2, 17, 12],
    [28, 0, 12, 9, 13, 3, 29, 24, 20, 6, 4, 7, 17, 21, 25, 26, 2, 18, 8, 15, 5, 19, 27, 22, 30, 14, 16, 10, 11, 31, 1, 23],
    [3, 31, 2, 4, 14, 17, 5, 24, 29, 30, 0, 18, 8, 9, 7, 27, 1, 28, 26, 20, 16, 15, 19, 23, 25, 6, 10, 22, 12, 13, 21, 11],
    [19, 5, 25, 29, 0, 8, 4, 11, 7, 27, 31, 30, 24, 2, 18, 9, 17, 21, 1, 26, 28, 10, 14, 13, 22, 3, 23, 6, 20, 16, 12, 15],
]


def plan(ncore, ncol):
    pairs, pieces = [], []
    for s, line in enumerate(SERVES):
        for q, target in enumerate(line):
            r, h = divmod(target, 2)
            pairs.append((s * ncol + q, r * ncol + 2 * s + h))
            pieces.append(h * ncore + r % ncore)
    return pairs, pieces


def piece_kernel(device_ref, at_ref, mask_ref, factor_ref, out_ref):
    rows, width = factor_ref.shape[1:]
    block = at_ref[device_ref[0]] * (rows // 128)
    for k in range(2):
        for i in range(rows // 128):
            kept = jnp.where(mask_ref[k, block + i] == 1, factor_ref[k, i * 128 : i * 128 + 128, :], 0.0)
            out_ref[i * 128 : i * 128 + 128, k * width : k * width + width] = kept.astype(jnp.bfloat16)


def product_kernel(mask_ref, core_ref, same_ref, other_ref, inverse_ref, out_ref, turned, product):
    width = same_ref.shape[1] // 2
    rows, cols = inverse_ref.shape
    first = core_ref[0] == 0
    turned[:, : cols // 2] = jnp.where(first, same_ref[...], other_ref[...]).T
    turned[:, cols // 2 :] = jnp.where(first, other_ref[...], same_ref[...]).T
    step = 256
    for i in range(rows // step):
        blocks = []
        for j in range(cols // 128):
            column = [
                jnp.where(
                    mask_ref[i * step // 128 + h, j] == 1,
                    inverse_ref[i * step + h * 128 : i * step + h * 128 + 128, j * 128 : j * 128 + 128],
                    0.0,
                ).astype(jnp.bfloat16)
                for h in range(step // 128)
            ]
            blocks.append(jnp.concatenate(column, axis=0))
        masked = jnp.concatenate(blocks, axis=1)
        product[:, i * step : i * step + step] = dot(turned[...], masked, 1, 1)
    count = out_ref.shape[1]
    for x in range(out_ref.shape[0]):
        body, code = encode_rows(
            product[x * count : x * count + count, :],
            product[width + x * count : width + x * count + count, :],
        )
        out_ref[x, :, :rows] = body
        out_ref[x, :, rows:] = code


def middle_kernel(in_ref, out_ref):
    rows = in_ref.shape[2] - 128
    high, low = decode_rows(in_ref, 0, rows)
    for i in range(1, in_ref.shape[0]):
        more_high, more_low = decode_rows(in_ref, i, rows)
        high, low = high + more_high, low + more_low
    body, code = encode_rows(high, low)
    out_ref[:, :rows] = body
    out_ref[:, rows:] = code


def encode_grams(grams, store):
    for k, gram in enumerate(grams):
        half = gram.shape[1] // 2
        top = jnp.max(jnp.max(jnp.abs(gram), axis=1, keepdims=True), axis=0, keepdims=True)
        step, code = scale_of(jnp.broadcast_to(top, (1, half)))
        inverse = LIMIT / step
        store(k, join(whole(gram[:, :half], inverse), whole(gram[:, half:], inverse)), code)


def place_rows(high, low, fixed_ref, code_ref):
    top = jnp.max(jnp.maximum(jnp.abs(high), jnp.abs(low)), axis=1, keepdims=True)
    step, code = scale_of(jnp.broadcast_to(jnp.max(top, axis=0, keepdims=True), (1, 128)))
    code_ref[...] = code
    inverse = (FIXED / step)[:, :1]
    parts = [whole(v, inverse)[h * 4 : h * 4 + 4] for h in range(2) for v in (high, low)]
    lane = lax.broadcasted_iota(jnp.int32, (4, 128), 1) // 32
    for tile in range(high.shape[1] // 128):
        pieces = [p[:, tile * 128 : tile * 128 + 128] for p in parts]
        turned = [[p if s == 0 else pltpu.roll(p, 32 * s, 1) for s in range(4)] for p in pieces]
        for quarter in range(4):
            found = turned[0][-quarter % 4]
            for b in range(1, 4):
                found = jnp.where(lane == b, turned[b][(b - quarter) % 4], found)
            fixed_ref[tile * 4 + quarter] = found


def gram_kernel(mask_ref, in_ref, factor_ref, out_ref, fixed_ref, code_ref):
    rows = in_ref.shape[2] - 128
    slot = in_ref.shape[1]
    high, low = decode_rows(in_ref, 0, rows)
    for i in range(1, in_ref.shape[0]):
        more_high, more_low = decode_rows(in_ref, i, rows)
        high, low = high + more_high, low + more_low
    place_rows(high, low, fixed_ref, code_ref)
    pieces = jnp.concatenate([p.astype(jnp.float32) for p in split(high) + split(low)], axis=0)
    pieces = pieces.astype(jnp.bfloat16)
    sums = []
    for k in range(2):
        panel = jnp.concatenate(
            [
                jnp.where(mask_ref[k, i] == 1, factor_ref[k, i * 128 : i * 128 + 128, :], 0.0).astype(jnp.bfloat16)
                for i in range(rows // 128)
            ],
            axis=0,
        )
        found = dot(pieces, panel, 1, 0)
        for s in range(2):
            b = 3 * slot * s
            sums.append(
                found[b : b + slot] + found[b + slot : b + 2 * slot] + found[b + 2 * slot : b + 3 * slot]
            )
    half = sums[0].shape[1] // 2

    def store(k, body, code):
        for r in range(out_ref.shape[0]):
            out_ref[r, k * slot : k * slot + slot, :] = body
            out_ref[r, 3 * slot + k : 3 * slot + k + 1, :] = code

    filler = jnp.zeros((out_ref.shape[1] - 3 * slot - 3, half), jnp.int32)
    for r in range(out_ref.shape[0]):
        out_ref[r, 3 * slot + 3 :, :] = filler
    encode_grams((sums[0], sums[2], sums[3]), store)


def decode_gram(ref, index, k, slot):
    high, low = part(ref[index, k * slot : k * slot + slot, :])
    unit = scale_from(ref[index, 3 * slot + k : 3 * slot + k + 1, :]) * (1.0 / LIMIT)
    return jnp.concatenate([high * unit, low * unit], axis=1)


def spread_kernel(in_ref, fixed_ref, code_ref, out_ref):
    slot = (in_ref.shape[1] - 8) // 3
    grams = []
    for k in range(3):
        gram = decode_gram(in_ref, 0, k, slot)
        for i in range(1, in_ref.shape[0]):
            gram = gram + decode_gram(in_ref, i, k, slot)
        grams.append(gram)

    def store(k, body, code):
        for c in range(out_ref.shape[0]):
            out_ref[c, k * slot : k * slot + slot, :] = body
            out_ref[c, 3 * slot + k : 3 * slot + k + 1, :] = code

    encode_grams(grams, store)
    for c in range(out_ref.shape[0]):
        out_ref[c, 3 * slot + 3 : 3 * slot + 4, :] = code_ref[...]
        out_ref[c, 3 * slot + 4 :, :] = fixed_ref[c]


def exact(a, b, ca, cb):
    parts = split(a)
    return dot(parts[0], b, ca, cb) + (dot(parts[1], b, ca, cb) + dot(parts[2], b, ca, cb))


def final_kernel(in_ref, top_ref, pivots_ref, parent_column, parent_diag, child_upper, child_column, child_diag):
    ncol = in_ref.shape[0]
    width = top_ref.shape[0]
    slot = width // ncol
    top = top_ref[...]
    grams = []
    for k in range(3):
        high, low = part(in_ref[:, k * slot : k * slot + slot, :])
        unit = scale_from(in_ref[:, 3 * slot + k : 3 * slot + k + 1, :]) * (1.0 / LIMIT)
        high = (high * unit).reshape(width, width // 2)
        grams.append(jnp.concatenate([high, (low * unit).reshape(width, width // 2)], axis=1))
    diag = pivots_ref[0] + grams[0].T
    parent_diag[...] = diag
    upper = grams[1] - exact(diag, top, 1, 0)
    child_upper[...] = upper
    parts = split(upper)
    turned = dot(top, parts[0], 0, 0) + (dot(top, parts[1], 0, 0) + dot(top, parts[2], 0, 0))
    child_diag[...] = pivots_ref[1] - turned - exact(grams[1], top, 0, 0) + grams[2].T

    unit = scale_from(in_ref[:, 3 * slot + 3 : 3 * slot + 4, :]) * (1.0 / FIXED)
    count = ncol * slot // 2
    sums = (in_ref[:, 3 * slot + 4 :, :].astype(jnp.float32) * unit).reshape(count, 128)
    row = lax.broadcasted_iota(jnp.int32, (count, width), 0)
    column = lax.broadcasted_iota(jnp.int32, (count, width), 1)
    placed = None
    for h in range(2):
        choice = jnp.where(column == slot * (row // 4) + 4 * h + row % 4, 1.0, 0.0).astype(jnp.bfloat16)
        for piece in split(sums):
            term = dot(piece, choice, 0, 0)[64 * h : 64 * h + 64]
            placed = term if placed is None else placed + term
    own = placed.shape[0] // 2
    parent_column[...] = -placed[:own]
    child_column[...] = exact(placed[:own], top, 1, 0) - placed[own:]


def call(kernel, out_shape, smem=0, scratch=(), results=pltpu.VMEM, name=None):
    single = isinstance(out_shape, jax.ShapeDtypeStruct)
    shapes = [out_shape] if single else list(out_shape)
    if results is not None:
        shapes = [results(s.shape, s.dtype) for s in shapes]

    def run(*args):
        found = pl.pallas_call(
            kernel,
            out_shape=shapes,
            in_specs=[SMEM] * smem + [VMEM] * (len(args) - smem),
            out_specs=[VMEM] * len(shapes),
            scratch_shapes=list(scratch),
            name=name,
        )(*args[:smem], *(pltpu.with_memory_space_constraint(a, pltpu.VMEM) for a in args[smem:]))
        return found[0] if single else found

    return run


def shards(inverse_block, tile_mask, factor, panel_mask, child_top, pivots):
    rows, cols = inverse_block.shape
    width = factor.shape[2]
    ncore = lax.axis_size("core")
    nrow = lax.axis_size("y") * ncore
    nx, nz = lax.axis_size("x"), lax.axis_size("z")
    ncol = nx * nz
    piece = cols // ncore
    own_rows = rows // ncol
    slot = width // ncol
    i32 = lambda *shape: jax.ShapeDtypeStruct(shape, jnp.int32)
    f32 = lambda *shape: jax.ShapeDtypeStruct(shape, jnp.float32)

    pairs, pieces = plan(ncore, ncol)
    sent = pl.pallas_call(
        piece_kernel,
        out_shape=pltpu.VMEM((piece, 2 * width), jnp.bfloat16),
        grid_spec=pltpu.PrefetchScalarGridSpec(
            num_scalar_prefetch=3,
            grid=(1,),
            in_specs=[pl.BlockSpec((2, piece, width), lambda i, device, at, mask: (0, at[device[0]], 0))],
            out_specs=VMEM,
        ),
        name="piece",
    )(lax.axis_index(ROW + COL).reshape(1), jnp.array(pieces, jnp.int32), panel_mask, factor)
    same = lax.ppermute(sent, ROW + COL, pairs)
    other = lax.ppermute(same, "core", [(0, 1), (1, 0)])

    coded = call(
        product_kernel,
        i32(nx, nz * slot, rows + 128),
        smem=2,
        scratch=[pltpu.VMEM((2 * width, cols), jnp.bfloat16), pltpu.VMEM((2 * width, rows), jnp.float32)],
        name="product",
    )(tile_mask, lax.axis_index("core").reshape(1), same, other, inverse_block)
    coded = lax.all_to_all(coded, "x", 0, 0, tiled=True)
    coded = call(middle_kernel, i32(nz * slot, rows + 128), name="middle")(coded)
    coded = lax.all_to_all(coded.reshape(nz, slot, rows + 128), "z", 0, 0, tiled=True)
    gram, fixed, code = call(
        gram_kernel,
        (i32(nrow, 3 * slot + 8, width // 2), i32(ncol, slot // 2, 128), i32(1, 128)),
        smem=1,
        name="gram",
    )(panel_mask, coded, factor)
    gram = lax.all_to_all(gram, ROW, 0, 0, tiled=True)

    last = call(spread_kernel, i32(ncol, 3 * slot + 8, width // 2), name="spread")(
        gram, fixed, code
    )
    last = lax.all_to_all(last, COL, 0, 0, tiled=True)
    return tuple(
        call(
            final_kernel,
            (f32(own_rows, width), f32(width, width), f32(width, width), f32(own_rows, width), f32(width, width)),
            results=None,
            name="final",
        )(last, child_top, pivots)
    )


def solution(mesh):
    grid = Mesh(mesh.devices.reshape(8, 2, 4, 8), ROW + COL)
    in_specs = (P(ROW, COL), P(ROW, COL), P(None, ROW, None), P(None, ROW), P(), P())
    out_specs = (P(ROW + COL, None), P(), P(), P(ROW + COL, None), P())
    return jax.shard_map(shards, mesh=grid, in_specs=in_specs, out_specs=out_specs, check_vma=False)
```

```python
import jax
import jax.numpy as jnp
from jax import lax
from jax.experimental import pallas as pl
from jax.experimental.pallas import tpu as pltpu
from jax.sharding import Mesh, PartitionSpec as P

ROW = ("y", "core")
COL = ("x", "z")
LIMIT = 32766.0
FIXED = float(1 << 30)
VMEM = pl.BlockSpec(memory_space=pltpu.VMEM)
SMEM = pl.BlockSpec(memory_space=pltpu.SMEM)


def scale_of(top):
    top = jnp.maximum(top, 1e-30)
    power = jnp.ceil(jnp.log2(top))
    mantissa = jnp.ceil(top * jnp.exp2(14.0 - power) + 2.0)
    code = (power.astype(jnp.int32) << 16) | mantissa.astype(jnp.int32)
    return mantissa * jnp.exp2(power - 14.0), code


def scale_from(code):
    return (code & 0xFFFF).astype(jnp.float32) * jnp.exp2((code >> 16).astype(jnp.float32) - 14.0)


def whole(value, factor):
    return jnp.round(value * factor).astype(jnp.int32)


def join(high, low):
    return (high << 16) | (low & 0xFFFF)


def part(joined):
    return (joined >> 16).astype(jnp.float32), ((joined << 16) >> 16).astype(jnp.float32)


def split(value):
    high = value.astype(jnp.bfloat16)
    rest = value - high.astype(jnp.float32)
    middle = rest.astype(jnp.bfloat16)
    return high, middle, (rest - middle.astype(jnp.float32)).astype(jnp.bfloat16)


def dot(a, b, ca, cb):
    return lax.dot_general(a, b, (((ca,), (cb,)), ((), ())), preferred_element_type=jnp.float32)


def encode_rows(high, low):
    high_step, high_code = scale_of(jnp.max(jnp.abs(high), axis=1, keepdims=True))
    low_step, low_code = scale_of(jnp.max(jnp.abs(low), axis=1, keepdims=True))
    body = join(whole(high, LIMIT / high_step), whole(low, LIMIT / low_step))
    lane = lax.broadcasted_iota(jnp.int32, (high.shape[0], 128), 1)
    return body, jnp.where(lane < 64, high_code, low_code)


def decode_rows(ref, index, rows):
    high, low = part(ref[index, :, :rows])
    code = ref[index, :, rows:]
    return high * (scale_from(code[:, :1]) * (1.0 / LIMIT)), low * (scale_from(code[:, 64:65]) * (1.0 / LIMIT))


SERVES = [
    [27, 9, 21, 15, 11, 6, 12, 1, 28, 18, 19, 5, 23, 24, 8, 4, 20, 26, 13, 29, 3, 2, 14, 16, 0, 17, 10, 31, 7, 30, 25, 22],
    [14, 21, 5, 1, 19, 27, 11, 26, 10, 8, 17, 24, 2, 6, 29, 16, 4, 18, 22, 9, 15, 23, 31, 28, 30, 12, 20, 7, 3, 13, 25, 0],
    [3, 0, 24, 28, 4, 17, 20, 21, 9, 2, 10, 12, 18, 31, 5, 19, 11, 6, 30, 14, 26, 27, 23, 1, 7, 8, 16, 29, 22, 25, 13, 15],
    [21, 30, 19, 4, 28, 20, 24, 18, 27, 31, 3, 8, 6, 16, 13, 5, 17, 7, 9, 0, 14, 12, 26, 23, 15, 1, 29, 10, 11, 2, 22, 25],
    [2, 27, 3, 31, 5, 12, 16, 8, 26, 25, 29, 13, 19, 0, 20, 28, 30, 23, 17, 6, 7, 4, 22, 10, 24, 21, 15, 11, 1, 18, 14, 9],
    [6, 17, 20, 24, 21, 2, 7, 28, 18, 22, 15, 31, 1, 13, 29, 14, 12, 30, 26, 27, 11, 19, 5, 8, 16, 10, 3, 25, 23, 4, 9, 0],
    [9, 10, 5, 22, 12, 21, 25, 18, 7, 4, 16, 26, 28, 31, 27, 3, 23, 8, 0, 20, 24, 29, 15, 13, 17, 6, 14, 2, 30, 11, 1, 19],
    [17, 21, 11, 26, 8, 0, 7, 1, 9, 12, 5, 22, 2, 14, 29, 27, 6, 23, 13, 10, 30, 24, 18, 15, 3, 31, 19, 16, 4, 28, 20, 25],
    [31, 7, 15, 19, 27, 10, 22, 30, 14, 23, 13, 9, 11, 24, 16, 2, 1, 8, 26, 20, 21, 12, 6, 0, 28, 29, 3, 25, 17, 18, 4, 5],
    [8, 26, 29, 9, 1, 15, 17, 16, 28, 6, 2, 3, 21, 11, 13, 12, 22, 0, 14, 5, 10, 18, 27, 24, 30, 4, 23, 7, 19, 25, 31, 20],
    [15, 28, 18, 20, 8, 7, 29, 27, 23, 24, 14, 4, 25, 3, 19, 9, 17, 26, 16, 30, 2, 10, 11, 5, 21, 22, 6, 0, 12, 13, 31, 1],
    [7, 15, 27, 12, 18, 28, 6, 9, 17, 13, 25, 16, 14, 8, 5, 29, 26, 1, 31, 24, 22, 30, 4, 19, 11, 3, 21, 20, 0, 2, 23, 10],
    [16, 17, 1, 7, 23, 26, 2, 6, 10, 0, 3, 21, 25, 30, 20, 4, 14, 29, 9, 19, 27, 18, 24, 31, 11, 13, 5, 22, 15, 12, 8, 28],
    [3, 6, 14, 11, 30, 31, 13, 22, 23, 0, 25, 7, 5, 17, 27, 26, 2, 16, 4, 8, 15, 29, 1, 20, 12, 18, 19, 10, 28, 9, 21, 24],
    [5, 14, 8, 19, 2, 4, 29, 1, 3, 28, 0, 22, 16, 11, 13, 23, 27, 12, 20, 18, 6, 15, 17, 31, 25, 24, 30, 26, 10, 21, 7, 9],
    [27, 1, 29, 0, 21, 16, 19, 15, 17, 23, 31, 30, 4, 20, 22, 24, 13, 28, 3, 6, 18, 10, 8, 9, 11, 5, 25, 12, 26, 7, 2, 14],
]


def plan(ncore, ncol):
    pairs, pieces = [], []
    for s, line in enumerate(SERVES):
        for q, target in enumerate(line):
            r, h = divmod(target, 2)
            pairs.append((s * ncol + q, r * ncol + 2 * s + h))
            pieces.append(h * ncore + r % ncore)
    return pairs, pieces


def piece_kernel(device_ref, at_ref, mask_ref, factor_ref, out_ref):
    rows, width = factor_ref.shape[1:]
    block = at_ref[device_ref[0]] * (rows // 128)
    for k in range(2):
        for i in range(rows // 128):
            kept = jnp.where(mask_ref[k, block + i] == 1, factor_ref[k, i * 128 : i * 128 + 128, :], 0.0)
            out_ref[i * 128 : i * 128 + 128, k * width : k * width + width] = kept.astype(jnp.bfloat16)


def product_kernel(mask_ref, core_ref, same_ref, other_ref, inverse_ref, out_ref, turned, product):
    width = same_ref.shape[1] // 2
    rows, cols = inverse_ref.shape
    first = core_ref[0] == 0
    turned[:, : cols // 2] = jnp.where(first, same_ref[...], other_ref[...]).T
    turned[:, cols // 2 :] = jnp.where(first, other_ref[...], same_ref[...]).T
    step = 256
    for i in range(rows // step):
        blocks = []
        for j in range(cols // 128):
            column = [
                jnp.where(
                    mask_ref[i * step // 128 + h, j] == 1,
                    inverse_ref[i * step + h * 128 : i * step + h * 128 + 128, j * 128 : j * 128 + 128],
                    0.0,
                ).astype(jnp.bfloat16)
                for h in range(step // 128)
            ]
            blocks.append(jnp.concatenate(column, axis=0))
        masked = jnp.concatenate(blocks, axis=1)
        product[:, i * step : i * step + step] = dot(turned[...], masked, 1, 1)
    count = out_ref.shape[1]
    for x in range(out_ref.shape[0]):
        body, code = encode_rows(
            product[x * count : x * count + count, :],
            product[width + x * count : width + x * count + count, :],
        )
        out_ref[x, :, :rows] = body
        out_ref[x, :, rows:] = code


def middle_kernel(in_ref, out_ref):
    rows = in_ref.shape[2] - 128
    high, low = decode_rows(in_ref, 0, rows)
    for i in range(1, in_ref.shape[0]):
        more_high, more_low = decode_rows(in_ref, i, rows)
        high, low = high + more_high, low + more_low
    body, code = encode_rows(high, low)
    out_ref[:, :rows] = body
    out_ref[:, rows:] = code


def encode_grams(grams, store):
    for k, gram in enumerate(grams):
        half = gram.shape[1] // 2
        top = jnp.max(jnp.max(jnp.abs(gram), axis=1, keepdims=True), axis=0, keepdims=True)
        step, code = scale_of(jnp.broadcast_to(top, (1, half)))
        inverse = LIMIT / step
        store(k, join(whole(gram[:, :half], inverse), whole(gram[:, half:], inverse)), code)


def place_rows(high, low, fixed_ref, code_ref):
    top = jnp.max(jnp.maximum(jnp.abs(high), jnp.abs(low)), axis=1, keepdims=True)
    step, code = scale_of(jnp.broadcast_to(jnp.max(top, axis=0, keepdims=True), (1, 128)))
    code_ref[...] = code
    inverse = (FIXED / step)[:, :1]
    parts = [whole(v, inverse)[h * 4 : h * 4 + 4] for h in range(2) for v in (high, low)]
    lane = lax.broadcasted_iota(jnp.int32, (4, 128), 1) // 32
    for tile in range(high.shape[1] // 128):
        pieces = [p[:, tile * 128 : tile * 128 + 128] for p in parts]
        turned = [[p if s == 0 else pltpu.roll(p, 32 * s, 1) for s in range(4)] for p in pieces]
        for quarter in range(4):
            found = turned[0][-quarter % 4]
            for b in range(1, 4):
                found = jnp.where(lane == b, turned[b][(b - quarter) % 4], found)
            fixed_ref[tile * 4 + quarter] = found


def gram_kernel(mask_ref, in_ref, factor_ref, out_ref, fixed_ref, code_ref):
    rows = in_ref.shape[2] - 128
    slot = in_ref.shape[1]
    high, low = decode_rows(in_ref, 0, rows)
    for i in range(1, in_ref.shape[0]):
        more_high, more_low = decode_rows(in_ref, i, rows)
        high, low = high + more_high, low + more_low
    place_rows(high, low, fixed_ref, code_ref)
    pieces = jnp.concatenate([p.astype(jnp.float32) for p in split(high) + split(low)], axis=0)
    pieces = pieces.astype(jnp.bfloat16)
    sums = []
    for k in range(2):
        panel = jnp.concatenate(
            [
                jnp.where(mask_ref[k, i] == 1, factor_ref[k, i * 128 : i * 128 + 128, :], 0.0).astype(jnp.bfloat16)
                for i in range(rows // 128)
            ],
            axis=0,
        )
        found = dot(pieces, panel, 1, 0)
        for s in range(2):
            b = 3 * slot * s
            sums.append(
                found[b : b + slot] + found[b + slot : b + 2 * slot] + found[b + 2 * slot : b + 3 * slot]
            )
    half = sums[0].shape[1] // 2

    def store(k, body, code):
        for r in range(out_ref.shape[0]):
            out_ref[r, k * slot : k * slot + slot, :] = body
            out_ref[r, 3 * slot + k : 3 * slot + k + 1, :] = code

    filler = jnp.zeros((out_ref.shape[1] - 3 * slot - 3, half), jnp.int32)
    for r in range(out_ref.shape[0]):
        out_ref[r, 3 * slot + 3 :, :] = filler
    encode_grams((sums[0], sums[2], sums[3]), store)


def decode_gram(ref, index, k, slot):
    high, low = part(ref[index, k * slot : k * slot + slot, :])
    unit = scale_from(ref[index, 3 * slot + k : 3 * slot + k + 1, :]) * (1.0 / LIMIT)
    return jnp.concatenate([high * unit, low * unit], axis=1)


def spread_kernel(in_ref, fixed_ref, code_ref, out_ref):
    slot = (in_ref.shape[1] - 8) // 3
    grams = []
    for k in range(3):
        gram = decode_gram(in_ref, 0, k, slot)
        for i in range(1, in_ref.shape[0]):
            gram = gram + decode_gram(in_ref, i, k, slot)
        grams.append(gram)

    def store(k, body, code):
        for c in range(out_ref.shape[0]):
            out_ref[c, k * slot : k * slot + slot, :] = body
            out_ref[c, 3 * slot + k : 3 * slot + k + 1, :] = code

    encode_grams(grams, store)
    for c in range(out_ref.shape[0]):
        out_ref[c, 3 * slot + 3 : 3 * slot + 4, :] = code_ref[...]
        out_ref[c, 3 * slot + 4 :, :] = fixed_ref[c]


def exact(a, b, ca, cb):
    parts = split(a)
    return dot(parts[0], b, ca, cb) + (dot(parts[1], b, ca, cb) + dot(parts[2], b, ca, cb))


def final_kernel(in_ref, top_ref, pivots_ref, parent_column, parent_diag, child_upper, child_column, child_diag):
    ncol = in_ref.shape[0]
    width = top_ref.shape[0]
    slot = width // ncol
    top = top_ref[...]
    grams = []
    for k in range(3):
        high, low = part(in_ref[:, k * slot : k * slot + slot, :])
        unit = scale_from(in_ref[:, 3 * slot + k : 3 * slot + k + 1, :]) * (1.0 / LIMIT)
        high = (high * unit).reshape(width, width // 2)
        grams.append(jnp.concatenate([high, (low * unit).reshape(width, width // 2)], axis=1))
    diag = pivots_ref[0] + grams[0].T
    parent_diag[...] = diag
    upper = grams[1] - exact(diag, top, 1, 0)
    child_upper[...] = upper
    parts = split(upper)
    turned = dot(top, parts[0], 0, 0) + (dot(top, parts[1], 0, 0) + dot(top, parts[2], 0, 0))
    child_diag[...] = pivots_ref[1] - turned - exact(grams[1], top, 0, 0) + grams[2].T

    unit = scale_from(in_ref[:, 3 * slot + 3 : 3 * slot + 4, :]) * (1.0 / FIXED)
    count = ncol * slot // 2
    sums = (in_ref[:, 3 * slot + 4 :, :].astype(jnp.float32) * unit).reshape(count, 128)
    row = lax.broadcasted_iota(jnp.int32, (count, width), 0)
    column = lax.broadcasted_iota(jnp.int32, (count, width), 1)
    placed = None
    for h in range(2):
        choice = jnp.where(column == slot * (row // 4) + 4 * h + row % 4, 1.0, 0.0).astype(jnp.bfloat16)
        for piece in split(sums):
            term = dot(piece, choice, 0, 0)[64 * h : 64 * h + 64]
            placed = term if placed is None else placed + term
    own = placed.shape[0] // 2
    parent_column[...] = -placed[:own]
    child_column[...] = exact(placed[:own], top, 1, 0) - placed[own:]


def call(kernel, out_shape, smem=0, scratch=(), results=pltpu.VMEM, name=None):
    single = isinstance(out_shape, jax.ShapeDtypeStruct)
    shapes = [out_shape] if single else list(out_shape)
    if results is not None:
        shapes = [results(s.shape, s.dtype) for s in shapes]

    def run(*args):
        found = pl.pallas_call(
            kernel,
            out_shape=shapes,
            in_specs=[SMEM] * smem + [VMEM] * (len(args) - smem),
            out_specs=[VMEM] * len(shapes),
            scratch_shapes=list(scratch),
            name=name,
        )(*args[:smem], *(pltpu.with_memory_space_constraint(a, pltpu.VMEM) for a in args[smem:]))
        return found[0] if single else found

    return run


def shards(inverse_block, tile_mask, factor, panel_mask, child_top, pivots):
    rows, cols = inverse_block.shape
    width = factor.shape[2]
    ncore = lax.axis_size("core")
    nrow = lax.axis_size("y") * ncore
    nx, nz = lax.axis_size("x"), lax.axis_size("z")
    ncol = nx * nz
    piece = cols // ncore
    own_rows = rows // ncol
    slot = width // ncol
    i32 = lambda *shape: jax.ShapeDtypeStruct(shape, jnp.int32)
    f32 = lambda *shape: jax.ShapeDtypeStruct(shape, jnp.float32)

    pairs, pieces = plan(ncore, ncol)
    sent = pl.pallas_call(
        piece_kernel,
        out_shape=pltpu.VMEM((piece, 2 * width), jnp.bfloat16),
        grid_spec=pltpu.PrefetchScalarGridSpec(
            num_scalar_prefetch=3,
            grid=(1,),
            in_specs=[pl.BlockSpec((2, piece, width), lambda i, device, at, mask: (0, at[device[0]], 0))],
            out_specs=VMEM,
        ),
        name="piece",
    )(lax.axis_index(ROW + COL).reshape(1), jnp.array(pieces, jnp.int32), panel_mask, factor)
    same = lax.ppermute(sent, ROW + COL, pairs)
    other = lax.ppermute(same, "core", [(0, 1), (1, 0)])

    coded = call(
        product_kernel,
        i32(nx, nz * slot, rows + 128),
        smem=2,
        scratch=[pltpu.VMEM((2 * width, cols), jnp.bfloat16), pltpu.VMEM((2 * width, rows), jnp.float32)],
        name="product",
    )(tile_mask, lax.axis_index("core").reshape(1), same, other, inverse_block)
    coded = lax.all_to_all(coded, "x", 0, 0, tiled=True)
    coded = call(middle_kernel, i32(nz * slot, rows + 128), name="middle")(coded)
    coded = lax.all_to_all(coded.reshape(nz, slot, rows + 128), "z", 0, 0, tiled=True)
    gram, fixed, code = call(
        gram_kernel,
        (i32(nrow, 3 * slot + 8, width // 2), i32(ncol, slot // 2, 128), i32(1, 128)),
        smem=1,
        name="gram",
    )(panel_mask, coded, factor)
    gram = lax.all_to_all(gram, ROW, 0, 0, tiled=True)

    last = call(spread_kernel, i32(ncol, 3 * slot + 8, width // 2), name="spread")(
        gram, fixed, code
    )
    last = lax.all_to_all(last, COL, 0, 0, tiled=True)
    return tuple(
        call(
            final_kernel,
            (f32(own_rows, width), f32(width, width), f32(width, width), f32(own_rows, width), f32(width, width)),
            results=None,
            name="final",
        )(last, child_top, pivots)
    )


def solution(mesh):
    grid = Mesh(mesh.devices.reshape(8, 2, 4, 8), ROW + COL)
    in_specs = (P(ROW, COL), P(ROW, COL), P(None, ROW, None), P(None, ROW), P(), P())
    out_specs = (P(ROW + COL, None), P(), P(), P(ROW + COL, None), P())
    return jax.shard_map(shards, mesh=grid, in_specs=in_specs, out_specs=out_specs, check_vma=False)
```

```python
import jax
import jax.numpy as jnp
from jax import lax
from jax.experimental import pallas as pl
from jax.experimental.pallas import tpu as pltpu
from jax.sharding import Mesh, PartitionSpec as P

ROW = ("y", "core")
COL = ("x", "z")
LIMIT = 32766.0
FIXED = float(1 << 30)
VMEM = pl.BlockSpec(memory_space=pltpu.VMEM)
SMEM = pl.BlockSpec(memory_space=pltpu.SMEM)


def scale_of(top):
    top = jnp.maximum(top, 1e-30)
    power = jnp.ceil(jnp.log2(top))
    mantissa = jnp.ceil(top * jnp.exp2(14.0 - power) + 2.0)
    code = (power.astype(jnp.int32) << 16) | mantissa.astype(jnp.int32)
    return mantissa * jnp.exp2(power - 14.0), code


def scale_from(code):
    return (code & 0xFFFF).astype(jnp.float32) * jnp.exp2((code >> 16).astype(jnp.float32) - 14.0)


def whole(value, factor):
    return jnp.round(value * factor).astype(jnp.int32)


def join(high, low):
    return (high << 16) | (low & 0xFFFF)


def part(joined):
    return (joined >> 16).astype(jnp.float32), ((joined << 16) >> 16).astype(jnp.float32)


def split(value):
    high = value.astype(jnp.bfloat16)
    rest = value - high.astype(jnp.float32)
    middle = rest.astype(jnp.bfloat16)
    return high, middle, (rest - middle.astype(jnp.float32)).astype(jnp.bfloat16)


def dot(a, b, ca, cb):
    return lax.dot_general(a, b, (((ca,), (cb,)), ((), ())), preferred_element_type=jnp.float32)


def encode_pair(high, low):
    high_step, high_code = scale_of(jnp.max(jnp.abs(high), axis=1, keepdims=True))
    low_step, low_code = scale_of(jnp.max(jnp.abs(low), axis=1, keepdims=True))
    return join(whole(high, LIMIT / high_step), whole(low, LIMIT / low_step)), high_code, low_code


def encode_rows(high, low):
    body, high_code, low_code = encode_pair(high, low)
    lane = lax.broadcasted_iota(jnp.int32, (high.shape[0], 128), 1)
    return body, jnp.where(lane < 64, high_code, low_code)


def diagonal(count):
    shape = (count, 128)
    return lax.broadcasted_iota(jnp.int32, shape, 0), lax.broadcasted_iota(jnp.int32, shape, 1)


def decode_tiles(ref, index, count):
    tiles = ref.shape[1] // count
    body = [ref[index, j * count : j * count + count, :] for j in range(tiles)]
    high, low = part(jnp.concatenate(body, axis=1))
    unit = scale_from(ref[index, tiles * count : tiles * count + 1, :]) * (1.0 / LIMIT)
    row, lane = diagonal(count)
    high_unit = jnp.sum(jnp.where(lane == row, unit, 0.0), axis=1, keepdims=True)
    low_unit = jnp.sum(jnp.where(lane == row + 64, unit, 0.0), axis=1, keepdims=True)
    return high * high_unit, low * low_unit


def decode_rows(ref, index, rows):
    high, low = part(ref[index, :, :rows])
    code = ref[index, :, rows:]
    return high * (scale_from(code[:, :1]) * (1.0 / LIMIT)), low * (scale_from(code[:, 64:65]) * (1.0 / LIMIT))


SERVES = [
    [27, 9, 21, 15, 11, 6, 12, 1, 28, 18, 19, 5, 23, 24, 8, 4, 20, 26, 13, 29, 3, 2, 14, 16, 0, 17, 10, 31, 7, 30, 25, 22],
    [14, 21, 5, 1, 19, 27, 11, 26, 10, 8, 17, 24, 2, 6, 29, 16, 4, 18, 22, 9, 15, 23, 31, 28, 30, 12, 20, 7, 3, 13, 25, 0],
    [3, 0, 24, 28, 4, 17, 20, 21, 9, 2, 10, 12, 18, 31, 5, 19, 11, 6, 30, 14, 26, 27, 23, 1, 7, 8, 16, 29, 22, 25, 13, 15],
    [21, 30, 19, 4, 28, 20, 24, 18, 27, 31, 3, 8, 6, 16, 13, 5, 17, 7, 9, 0, 14, 12, 26, 23, 15, 1, 29, 10, 11, 2, 22, 25],
    [2, 27, 3, 31, 5, 12, 16, 8, 26, 25, 29, 13, 19, 0, 20, 28, 30, 23, 17, 6, 7, 4, 22, 10, 24, 21, 15, 11, 1, 18, 14, 9],
    [6, 17, 20, 24, 21, 2, 7, 28, 18, 22, 15, 31, 1, 13, 29, 14, 12, 30, 26, 27, 11, 19, 5, 8, 16, 10, 3, 25, 23, 4, 9, 0],
    [9, 10, 5, 22, 12, 21, 25, 18, 7, 4, 16, 26, 28, 31, 27, 3, 23, 8, 0, 20, 24, 29, 15, 13, 17, 6, 14, 2, 30, 11, 1, 19],
    [17, 21, 11, 26, 8, 0, 7, 1, 9, 12, 5, 22, 2, 14, 29, 27, 6, 23, 13, 10, 30, 24, 18, 15, 3, 31, 19, 16, 4, 28, 20, 25],
    [31, 7, 15, 19, 27, 10, 22, 30, 14, 23, 13, 9, 11, 24, 16, 2, 1, 8, 26, 20, 21, 12, 6, 0, 28, 29, 3, 25, 17, 18, 4, 5],
    [8, 26, 29, 9, 1, 15, 17, 16, 28, 6, 2, 3, 21, 11, 13, 12, 22, 0, 14, 5, 10, 18, 27, 24, 30, 4, 23, 7, 19, 25, 31, 20],
    [15, 28, 18, 20, 8, 7, 29, 27, 23, 24, 14, 4, 25, 3, 19, 9, 17, 26, 16, 30, 2, 10, 11, 5, 21, 22, 6, 0, 12, 13, 31, 1],
    [7, 15, 27, 12, 18, 28, 6, 9, 17, 13, 25, 16, 14, 8, 5, 29, 26, 1, 31, 24, 22, 30, 4, 19, 11, 3, 21, 20, 0, 2, 23, 10],
    [16, 17, 1, 7, 23, 26, 2, 6, 10, 0, 3, 21, 25, 30, 20, 4, 14, 29, 9, 19, 27, 18, 24, 31, 11, 13, 5, 22, 15, 12, 8, 28],
    [3, 6, 14, 11, 30, 31, 13, 22, 23, 0, 25, 7, 5, 17, 27, 26, 2, 16, 4, 8, 15, 29, 1, 20, 12, 18, 19, 10, 28, 9, 21, 24],
    [5, 14, 8, 19, 2, 4, 29, 1, 3, 28, 0, 22, 16, 11, 13, 23, 27, 12, 20, 18, 6, 15, 17, 31, 25, 24, 30, 26, 10, 21, 7, 9],
    [27, 1, 29, 0, 21, 16, 19, 15, 17, 23, 31, 30, 4, 20, 22, 24, 13, 28, 3, 6, 18, 10, 8, 9, 11, 5, 25, 12, 26, 7, 2, 14],
]


def plan(ncore, ncol):
    pairs, pieces = [], []
    for s, line in enumerate(SERVES):
        for q, target in enumerate(line):
            r, h = divmod(target, 2)
            pairs.append((s * ncol + q, r * ncol + 2 * s + h))
            pieces.append(h * ncore + r % ncore)
    return pairs, pieces


def piece_kernel(device_ref, at_ref, mask_ref, factor_ref, out_ref):
    rows, width = factor_ref.shape[1:]
    block = at_ref[device_ref[0]] * (rows // 128)
    for k in range(2):
        for i in range(rows // 128):
            kept = jnp.where(mask_ref[k, block + i] == 1, factor_ref[k, i * 128 : i * 128 + 128, :], 0.0)
            out_ref[i * 128 : i * 128 + 128, k * width : k * width + width] = kept.astype(jnp.bfloat16)


def product_kernel(mask_ref, core_ref, same_ref, other_ref, inverse_ref, out_ref, turned, product):
    width = same_ref.shape[1] // 2
    rows, cols = inverse_ref.shape
    first = core_ref[0] == 0
    turned[:, : cols // 2] = jnp.where(first, same_ref[...], other_ref[...]).T
    turned[:, cols // 2 :] = jnp.where(first, other_ref[...], same_ref[...]).T
    step = 256
    for i in range(rows // step):
        blocks = []
        for j in range(cols // 128):
            column = [
                jnp.where(
                    mask_ref[i * step // 128 + h, j] == 1,
                    inverse_ref[i * step + h * 128 : i * step + h * 128 + 128, j * 128 : j * 128 + 128],
                    0.0,
                ).astype(jnp.bfloat16)
                for h in range(step // 128)
            ]
            blocks.append(jnp.concatenate(column, axis=0))
        masked = jnp.concatenate(blocks, axis=1)
        product[:, i * step : i * step + step] = dot(turned[...], masked, 1, 1)
    count = width // out_ref.shape[0]
    for x in range(out_ref.shape[0]):
        body, high_code, low_code = encode_pair(
            product[x * count : x * count + count, :],
            product[width + x * count : width + x * count + count, :],
        )
        for j in range(rows // 128):
            out_ref[x, j * count : j * count + count, :] = body[:, j * 128 : j * 128 + 128]
        row, lane = diagonal(count)
        codes = jnp.where(lane == row, high_code, 0) + jnp.where(lane == row + 64, low_code, 0)
        out_ref[x, rows // 128 * count :, :] = jnp.broadcast_to(jnp.sum(codes, axis=0, keepdims=True), (8, 128))


def middle_kernel(in_ref, out_ref):
    count, rows = out_ref.shape[0], out_ref.shape[1] - 128
    high, low = decode_tiles(in_ref, 0, count)
    for i in range(1, in_ref.shape[0]):
        more_high, more_low = decode_tiles(in_ref, i, count)
        high, low = high + more_high, low + more_low
    body, code = encode_rows(high, low)
    out_ref[:, :rows] = body
    out_ref[:, rows:] = code


def encode_grams(grams, store):
    for k, gram in enumerate(grams):
        half = gram.shape[1] // 2
        top = jnp.max(jnp.max(jnp.abs(gram), axis=1, keepdims=True), axis=0, keepdims=True)
        step, code = scale_of(jnp.broadcast_to(top, (1, half)))
        inverse = LIMIT / step
        store(k, join(whole(gram[:, :half], inverse), whole(gram[:, half:], inverse)), code)


def place_rows(high, low, fixed_ref, code_ref):
    top = jnp.max(jnp.maximum(jnp.abs(high), jnp.abs(low)), axis=1, keepdims=True)
    step, code = scale_of(jnp.broadcast_to(jnp.max(top, axis=0, keepdims=True), (1, 128)))
    code_ref[...] = code
    inverse = (FIXED / step)[:, :1]
    parts = [whole(v, inverse)[h * 4 : h * 4 + 4] for h in range(2) for v in (high, low)]
    lane = lax.broadcasted_iota(jnp.int32, (4, 128), 1) // 32
    for tile in range(high.shape[1] // 128):
        pieces = [p[:, tile * 128 : tile * 128 + 128] for p in parts]
        turned = [[p if s == 0 else pltpu.roll(p, 32 * s, 1) for s in range(4)] for p in pieces]
        for quarter in range(4):
            found = turned[0][-quarter % 4]
            for b in range(1, 4):
                found = jnp.where(lane == b, turned[b][(b - quarter) % 4], found)
            fixed_ref[tile * 4 + quarter] = found


def gram_kernel(mask_ref, in_ref, factor_ref, out_ref, fixed_ref, code_ref):
    rows = in_ref.shape[2] - 128
    slot = in_ref.shape[1]
    high, low = decode_rows(in_ref, 0, rows)
    for i in range(1, in_ref.shape[0]):
        more_high, more_low = decode_rows(in_ref, i, rows)
        high, low = high + more_high, low + more_low
    place_rows(high, low, fixed_ref, code_ref)
    pieces = jnp.concatenate([p.astype(jnp.float32) for p in split(high) + split(low)], axis=0)
    pieces = pieces.astype(jnp.bfloat16)
    sums = []
    for k in range(2):
        panel = jnp.concatenate(
            [
                jnp.where(mask_ref[k, i] == 1, factor_ref[k, i * 128 : i * 128 + 128, :], 0.0).astype(jnp.bfloat16)
                for i in range(rows // 128)
            ],
            axis=0,
        )
        found = dot(pieces, panel, 1, 0)
        for s in range(2):
            b = 3 * slot * s
            sums.append(
                found[b : b + slot] + found[b + slot : b + 2 * slot] + found[b + 2 * slot : b + 3 * slot]
            )
    half = sums[0].shape[1] // 2

    def store(k, body, code):
        for r in range(out_ref.shape[0]):
            out_ref[r, k * slot : k * slot + slot, :] = body
            out_ref[r, 3 * slot + k : 3 * slot + k + 1, :] = code

    filler = jnp.zeros((out_ref.shape[1] - 3 * slot - 3, half), jnp.int32)
    for r in range(out_ref.shape[0]):
        out_ref[r, 3 * slot + 3 :, :] = filler
    encode_grams((sums[0], sums[2], sums[3]), store)


def decode_gram(ref, index, k, slot):
    high, low = part(ref[index, k * slot : k * slot + slot, :])
    unit = scale_from(ref[index, 3 * slot + k : 3 * slot + k + 1, :]) * (1.0 / LIMIT)
    return jnp.concatenate([high * unit, low * unit], axis=1)


def spread_kernel(in_ref, fixed_ref, code_ref, out_ref):
    slot = (in_ref.shape[1] - 8) // 3
    grams = []
    for k in range(3):
        gram = decode_gram(in_ref, 0, k, slot)
        for i in range(1, in_ref.shape[0]):
            gram = gram + decode_gram(in_ref, i, k, slot)
        grams.append(gram)

    def store(k, body, code):
        for c in range(out_ref.shape[0]):
            out_ref[c, k * slot : k * slot + slot, :] = body
            out_ref[c, 3 * slot + k : 3 * slot + k + 1, :] = code

    encode_grams(grams, store)
    for c in range(out_ref.shape[0]):
        out_ref[c, 3 * slot + 3 : 3 * slot + 4, :] = code_ref[...]
        out_ref[c, 3 * slot + 4 :, :] = fixed_ref[c]


def exact(a, b, ca, cb):
    parts = split(a)
    return dot(parts[0], b, ca, cb) + (dot(parts[1], b, ca, cb) + dot(parts[2], b, ca, cb))


def final_kernel(in_ref, top_ref, pivots_ref, parent_column, parent_diag, child_upper, child_column, child_diag):
    ncol = in_ref.shape[0]
    width = top_ref.shape[0]
    slot = width // ncol
    top = top_ref[...]
    grams = []
    for k in range(3):
        high, low = part(in_ref[:, k * slot : k * slot + slot, :])
        unit = scale_from(in_ref[:, 3 * slot + k : 3 * slot + k + 1, :]) * (1.0 / LIMIT)
        high = (high * unit).reshape(width, width // 2)
        grams.append(jnp.concatenate([high, (low * unit).reshape(width, width // 2)], axis=1))
    diag = pivots_ref[0] + grams[0].T
    parent_diag[...] = diag
    upper = grams[1] - exact(diag, top, 1, 0)
    child_upper[...] = upper
    parts = split(upper)
    turned = dot(top, parts[0], 0, 0) + (dot(top, parts[1], 0, 0) + dot(top, parts[2], 0, 0))
    child_diag[...] = pivots_ref[1] - turned - exact(grams[1], top, 0, 0) + grams[2].T

    unit = scale_from(in_ref[:, 3 * slot + 3 : 3 * slot + 4, :]) * (1.0 / FIXED)
    count = ncol * slot // 2
    sums = (in_ref[:, 3 * slot + 4 :, :].astype(jnp.float32) * unit).reshape(count, 128)
    row = lax.broadcasted_iota(jnp.int32, (count, width), 0)
    column = lax.broadcasted_iota(jnp.int32, (count, width), 1)
    placed = None
    for h in range(2):
        choice = jnp.where(column == slot * (row // 4) + 4 * h + row % 4, 1.0, 0.0).astype(jnp.bfloat16)
        for piece in split(sums):
            term = dot(piece, choice, 0, 0)[64 * h : 64 * h + 64]
            placed = term if placed is None else placed + term
    own = placed.shape[0] // 2
    parent_column[...] = -placed[:own]
    child_column[...] = exact(placed[:own], top, 1, 0) - placed[own:]


def call(kernel, out_shape, smem=0, scratch=(), results=pltpu.VMEM, name=None):
    single = isinstance(out_shape, jax.ShapeDtypeStruct)
    shapes = [out_shape] if single else list(out_shape)
    if results is not None:
        shapes = [results(s.shape, s.dtype) for s in shapes]

    def run(*args):
        found = pl.pallas_call(
            kernel,
            out_shape=shapes,
            in_specs=[SMEM] * smem + [VMEM] * (len(args) - smem),
            out_specs=[VMEM] * len(shapes),
            scratch_shapes=list(scratch),
            name=name,
        )(*args[:smem], *(pltpu.with_memory_space_constraint(a, pltpu.VMEM) for a in args[smem:]))
        return found[0] if single else found

    return run


def shards(inverse_block, tile_mask, factor, panel_mask, child_top, pivots):
    rows, cols = inverse_block.shape
    width = factor.shape[2]
    ncore = lax.axis_size("core")
    nrow = lax.axis_size("y") * ncore
    nx, nz = lax.axis_size("x"), lax.axis_size("z")
    ncol = nx * nz
    piece = cols // ncore
    own_rows = rows // ncol
    slot = width // ncol
    i32 = lambda *shape: jax.ShapeDtypeStruct(shape, jnp.int32)
    f32 = lambda *shape: jax.ShapeDtypeStruct(shape, jnp.float32)

    pairs, pieces = plan(ncore, ncol)
    sent = pl.pallas_call(
        piece_kernel,
        out_shape=pltpu.VMEM((piece, 2 * width), jnp.bfloat16),
        grid_spec=pltpu.PrefetchScalarGridSpec(
            num_scalar_prefetch=3,
            grid=(1,),
            in_specs=[pl.BlockSpec((2, piece, width), lambda i, device, at, mask: (0, at[device[0]], 0))],
            out_specs=VMEM,
        ),
        name="piece",
    )(lax.axis_index(ROW + COL).reshape(1), jnp.array(pieces, jnp.int32), panel_mask, factor)
    same = lax.ppermute(sent, ROW + COL, pairs)
    other = lax.ppermute(same, "core", [(0, 1), (1, 0)])

    coded = call(
        product_kernel,
        i32(nx, nz * slot * (rows // 128) + 8, 128),
        smem=2,
        scratch=[pltpu.VMEM((2 * width, cols), jnp.bfloat16), pltpu.VMEM((2 * width, rows), jnp.float32)],
        name="product",
    )(tile_mask, lax.axis_index("core").reshape(1), same, other, inverse_block)
    coded = lax.all_to_all(coded, "x", 0, 0, tiled=True)
    coded = call(middle_kernel, i32(nz * slot, rows + 128), name="middle")(coded)
    coded = lax.all_to_all(coded.reshape(nz, slot, rows + 128), "z", 0, 0, tiled=True)
    gram, fixed, code = call(
        gram_kernel,
        (i32(nrow, 3 * slot + 8, width // 2), i32(ncol, slot // 2, 128), i32(1, 128)),
        smem=1,
        name="gram",
    )(panel_mask, coded, factor)
    gram = lax.all_to_all(gram, ROW, 0, 0, tiled=True)

    last = call(spread_kernel, i32(ncol, 3 * slot + 8, width // 2), name="spread")(
        gram, fixed, code
    )
    last = lax.all_to_all(last, COL, 0, 0, tiled=True)
    return tuple(
        call(
            final_kernel,
            (f32(own_rows, width), f32(width, width), f32(width, width), f32(own_rows, width), f32(width, width)),
            results=None,
            name="final",
        )(last, child_top, pivots)
    )


def solution(mesh):
    grid = Mesh(mesh.devices.reshape(8, 2, 4, 8), ROW + COL)
    in_specs = (P(ROW, COL), P(ROW, COL), P(None, ROW, None), P(None, ROW), P(), P())
    out_specs = (P(ROW + COL, None), P(), P(), P(ROW + COL, None), P())
    return jax.shard_map(shards, mesh=grid, in_specs=in_specs, out_specs=out_specs, check_vma=False)
```
